32 devices in a mesh: dp: 8 (over z, x), tensor: 4 (over y, core).
Axes of the slice: x: 2, y: 2, z: 4, core: 2. Of those that a mesh axis runs over, the one named last changes fastest.
Arguments:
- tokens: bfloat16 [8192, 2048], P(('dp', 'tensor')), may hold values from -6 to 6
- pieces: int32 [8192], P('dp'), may hold values from 0 to 32, as said below
- positions: int32 [8192], P('dp'), may hold values from 0 to 798, as said below
- cotangent: bfloat16 [8192, 2048], P(('dp', 'tensor')), may hold values from -6 to 6
- attn_norm: float32 [2048], P('dp'), may hold values from 0.25 to 1.75
- w_query: float32 [2048, 2048], P('dp', 'tensor'), may hold values from -0.125 to 0.125
- w_key: float32 [2048, 512], P('dp', 'tensor'), may hold values from -0.125 to 0.125
- w_value: float32 [2048, 512], P('dp', 'tensor'), may hold values from -0.125 to 0.125
- w_out: float32 [2048, 2048], P('tensor', 'dp'), may hold values from -0.75 to 0.75
- mlp_norm: float32 [2048], P('dp'), may hold values from 0.25 to 1.75
- w_gate: float32 [2048, 8192], P('dp', 'tensor'), may hold values from -0.125 to 0.125
- w_up: float32 [2048, 8192], P('dp', 'tensor'), may hold values from -0.125 to 0.125
- w_down: float32 [8192, 2048], P('tensor', 'dp'), may hold values from -0.0625 to 0.0625
Outputs:
- output: bfloat16 [8192, 2048], P(('dp', 'tensor'))
- input_grad: float32 [8192, 2048], P(('dp', 'tensor'))
- grad_attn_norm: float32 [2048], P('dp')
- grad_w_query: float32 [2048, 2048], P('dp', 'tensor')
- grad_w_key: float32 [2048, 512], P('dp', 'tensor')
- grad_w_value: float32 [2048, 512], P('dp', 'tensor')
- grad_w_out: float32 [2048, 2048], P('tensor', 'dp')
- grad_mlp_norm: float32 [2048], P('dp')
- grad_w_gate: float32 [2048, 8192], P('dp', 'tensor')
- grad_w_up: float32 [2048, 8192], P('dp', 'tensor')
- grad_w_down: float32 [8192, 2048], P('tensor', 'dp')
The draws below stay inside these ranges and needn't reach their ends.
Inputs may be any that keep to these rules, and one draw needn't show every extreme that they name: `pieces`: each aligned run of 256 tokens is text (0) or one picture piece numbered 1 + the run's index among all runs; the last run of every sequence is a picture piece. `positions`: A text token's position is its index within its sequence of 1024 tokens; the t-th token of a picture piece takes the index of the piece's first token + t // 16 + t % 16.
All inputs are finite; a program needn't handle non-finite values.
Results may differ from the reference program's by a relative error of at most 0.02.
Values may be sent and summed in bfloat16 or wider, within the bound.
No kernel may reach another device: no remote copies, remote signals or barrier semaphores. Data moves between devices by JAX's collectives and lax.ppermute only.
A program may use at most 256 MiB of HBM per device.

```python
import math
from functools import partial
import jax
import jax.numpy as jnp
from jax import lax

D = 2048
HEADS = 32
KV_HEADS = 8
HEAD_DIM = 64
FF = 8192
PIECE = 256
GRID = 16
SEQ = 1024
TOKENS = 8192


def picture_layout(key):
    slots = TOKENS // PIECE
    per_sequence = SEQ // PIECE
    picks = jax.random.randint(jax.random.fold_in(key, 7), (slots,), 0, 5)
    return (picks < 2) | (jnp.arange(slots) % per_sequence == per_sequence - 1)


def draw_pieces(key, part):
    picture = picture_layout(key)
    slots = picture.shape[0]
    numbers = jnp.where(picture, jnp.arange(1, slots + 1), 0).astype(jnp.int32)
    return jnp.repeat(numbers, PIECE)


def draw_positions(key, part):
    picture = picture_layout(key)
    inner = jnp.arange(PIECE)
    offsets = inner // GRID + inner % GRID
    per_sequence = SEQ // PIECE
    starts = (jnp.arange(per_sequence) * PIECE)[None, :, None]
    inside = jnp.where(picture.reshape(-1, per_sequence)[:, :, None], offsets[None, None, :], inner[None, None, :])
    return (starts + inside).reshape(-1).astype(jnp.int32)


def block_levels(own_key, shape, cuts, low, largest):
    def one(axis_at, blocks):
        draws = jax.random.uniform(jax.random.fold_in(jax.random.fold_in(own_key, 6), axis_at), (blocks,), jnp.float32, low / len(cuts), largest / len(cuts))
        return jnp.repeat(jnp.exp(draws), shape[axis_at] // blocks).reshape((-1,) + (1,) * (len(shape) - axis_at - 1))

    level = one(*cuts[0])
    for cut in cuts[1:]:
        level = level * one(*cut)
    return level


def normal_values(rng, extent, spread, reach, shards=(), kind=jnp.bfloat16):
    entries = jax.random.normal(rng, extent, jnp.float32) * spread
    if len(shards) > 0:
        entries = block_levels(rng, extent, shards, -0.22, 0.18) * entries
    return jnp.clip(entries, min=-reach, max=reach).astype(kind)


def setup_inputs(seed: int = 0) -> dict:
    splits = jax.random.split(jax.random.key(seed), 14)
    return {
        "tokens": normal_values(splits[0], (TOKENS, D), 1.0, 6.0, ((0, 32),)),
        "pieces": draw_pieces(jax.random.fold_in(splits[13], 71), 0),
        "positions": draw_positions(jax.random.fold_in(splits[13], 71), 0),
        "cotangent": normal_values(splits[3], (TOKENS, D), 1.0, 6.0, ((0, 32),)),
        "attn_norm": jnp.clip(1.0 + 0.15 * jax.random.normal(splits[4], (D,), jnp.float32), 0.25, 1.75),
        "w_query": normal_values(splits[5], (D, HEADS * HEAD_DIM), D ** -0.5, 0.125, ((0, 8), (1, 4)), jnp.float32),
        "w_key": normal_values(splits[6], (D, KV_HEADS * HEAD_DIM), D ** -0.5, 0.125, ((0, 8), (1, 4)), jnp.float32),
        "w_value": normal_values(splits[7], (D, KV_HEADS * HEAD_DIM), D ** -0.5, 0.125, ((0, 8), (1, 4)), jnp.float32),
        "w_out": normal_values(splits[8], (HEADS * HEAD_DIM, D), (HEADS * HEAD_DIM // 32) ** -0.5, 0.75, ((0, 4), (1, 8)), jnp.float32),
        "mlp_norm": jnp.clip(1.0 + 0.15 * jax.random.normal(splits[9], (D,), jnp.float32), 0.25, 1.75),
        "w_gate": normal_values(splits[10], (D, FF), D ** -0.5, 0.125, ((0, 8), (1, 4)), jnp.float32),
        "w_up": normal_values(splits[11], (D, FF), D ** -0.5, 0.125, ((0, 8), (1, 4)), jnp.float32),
        "w_down": normal_values(splits[12], (FF, D), FF ** -0.5, 0.0625, ((0, 4), (1, 8)), jnp.float32),
    }


@jax.custom_vjp
def low(v):
    return lax.optimization_barrier(v.astype(jnp.bfloat16)).astype(jnp.float32)

@jax.custom_vjp
def low_back(v):
    return v

def low_keep(v):
    return (low(v), None)

def low_pass(kept, grad):
    return (grad,)

def back_keep(v):
    return (v, None)

def back_low(kept, grad):
    return (low(grad),)
low.defvjp(low_keep, low_pass)
low_back.defvjp(back_keep, back_low)

def rotary_angles(positions, head_size):
    half = head_size // 2
    base = jnp.power(500000.0, -(jnp.arange(half, dtype=jnp.float32) * 2.0 / head_size))
    wavelen = 2.0 * math.pi / base
    smooth = (8192.0 / wavelen - 1.0) / 3.0
    blended = (1.0 - smooth) * base / 32.0 + smooth * base
    scaled = jnp.where(wavelen > 8192.0, base / 32.0, jnp.where(wavelen < 2048.0, base, blended))
    return positions.astype(jnp.float32)[:, None] * scaled[None, :]

def rotate(field, angles):
    half = field.shape[-1] // 2
    cosine = jnp.cos(angles)[:, None, :]
    sine = jnp.sin(angles)[:, None, :]
    first = field[..., :half]
    second = field[..., half:]
    return jnp.concatenate([first * cosine - second * sine, second * cosine + first * sine], axis=-1)

def product(left, right):
    return jnp.dot(left, right, precision=lax.Precision.HIGHEST)

def normalize(values, gain):
    inverse = lax.rsqrt(lax.optimization_barrier(jnp.mean(values * values, axis=-1, keepdims=True)) + 1e-05)
    return low(values * inverse * gain)

def one_sequence(span, pieces_row, positions_row, weights):
    attn_gain, query_weight, key_weight, value_weight, out_weight, mlp_gain, gate_weight, up_weight, down_weight = weights
    length = span.shape[0]
    group = HEADS // KV_HEADS
    normed = normalize(span, attn_gain)
    query = low_back(product(normed, query_weight)).reshape(length, HEADS, HEAD_DIM)
    keys = low_back(product(normed, key_weight)).reshape(length, KV_HEADS, HEAD_DIM)
    values = low_back(low(product(normed, value_weight))).reshape(length, KV_HEADS, HEAD_DIM)
    angles = rotary_angles(positions_row, HEAD_DIM)
    query = low(rotate(query, angles)).reshape(length, KV_HEADS, group, HEAD_DIM)
    keys = low(rotate(keys, angles))
    scores = low_back(jnp.einsum('qgrd,kgd->grqk', query, keys, precision=lax.Precision.HIGHEST) * HEAD_DIM ** (-0.5))
    rows = jnp.arange(length)[:, None]
    columns = jnp.arange(length)[None, :]
    owner = pieces_row[:, None]
    allowed = (columns <= rows) | (owner == pieces_row[None, :]) & (owner != 0)
    scores = jnp.where(allowed, scores, -1e+30)
    probs = low(jax.nn.softmax(scores, axis=-1))
    attended = low_back(low(jnp.einsum('grqk,kgd->qgrd', probs, values, precision=lax.Precision.HIGHEST)))
    attended = attended.reshape(length, HEADS * HEAD_DIM)
    middle = span + low_back(product(attended, out_weight))
    normed_two = normalize(middle, mlp_gain)
    gate = low_back(product(normed_two, gate_weight))
    up = low_back(product(normed_two, up_weight))
    hidden = low(jax.nn.silu(gate) * up)
    return middle + low_back(product(hidden, down_weight))

def forward(tokens32, attn_gain, query_weight, key_weight, value_weight, out_weight, mlp_gain, gate_weight, up_weight, down_weight, pieces, positions):
    weights = (low(attn_gain), low(query_weight), low(key_weight), low(value_weight), low(out_weight), low(mlp_gain), low(gate_weight), low(up_weight), low(down_weight))
    count = tokens32.shape[0] // SEQ

    def run(inputs):
        return one_sequence(inputs[0], inputs[1], inputs[2], weights)
    results = lax.map(jax.checkpoint(run), (tokens32.reshape(count, SEQ, D), pieces.reshape(count, SEQ), positions.reshape(count, SEQ)))
    return results.reshape(count * SEQ, D)

def reference(tokens, pieces, positions, cotangent, attn_norm, w_query, w_key, w_value, w_out, mlp_norm, w_gate, w_up, w_down):
    pulled = partial(forward, pieces=pieces, positions=positions)
    result, pullback = jax.vjp(pulled, tokens.astype(jnp.float32), attn_norm, w_query, w_key, w_value, w_out, mlp_norm, w_gate, w_up, w_down)
    grads = pullback(cotangent.astype(jnp.float32))
    return (result.astype(jnp.bfloat16), grads[0], grads[1], grads[2], grads[3], grads[4], grads[5], grads[6], grads[7], grads[8], grads[9])
```

```python
from functools import partial, reduce
import math

import jax
import jax.numpy as jnp
from jax import lax
from jax.sharding import PartitionSpec as P

HEADS = 32
KV_HEADS = 8
HEAD_DIM = 64


def rotary_angles(positions, head_size):
    half = head_size // 2
    base = jnp.power(500000.0, -(jnp.arange(half, dtype=jnp.float32) * 2.0 / head_size))
    wavelen = 2.0 * math.pi / base
    smooth = (8192.0 / wavelen - 1.0) / 3.0
    blended = (1.0 - smooth) * base / 32.0 + smooth * base
    scaled = jnp.where(wavelen > 8192.0, base / 32.0, jnp.where(wavelen < 2048.0, base, blended))
    return positions.astype(jnp.float32)[:, None] * scaled[None, :]


def rotate(field, angles):
    half = field.shape[-1] // 2
    cosine = jnp.cos(angles)[:, None, :]
    sine = jnp.sin(angles)[:, None, :]
    first = field[..., :half]
    second = field[..., half:]
    return jnp.concatenate(
        [first * cosine - second * sine, second * cosine + first * sine], axis=-1
    )


def normalize(residual, gain):
    inverse = lax.rsqrt(jnp.mean(residual * residual, axis=-1, keepdims=True) + 1e-05)
    return ((residual * inverse * gain.astype(jnp.float32)).astype(jnp.bfloat16), inverse)


def normalize_back(grad_normed, residual, inverse, gain):
    scaled = residual * inverse
    grad_gain = jnp.sum(grad_normed * scaled, axis=0)
    weighted = grad_normed * gain.astype(jnp.float32)
    grad_residual = inverse * (
        weighted - scaled * jnp.mean(weighted * scaled, axis=-1, keepdims=True)
    )
    return (grad_residual, grad_gain)


def row_product(left, right):
    return jnp.dot(left, right, preferred_element_type=jnp.float32)


def back_product(lefts, rights):
    parts = [
        lax.dot_general(left, right, (((1,), (1,)), ((), ())), preferred_element_type=jnp.float32)
        for left, right in zip(lefts, rights)
    ]
    return reduce(jnp.add, parts)


def across_rows(left, right):
    return lax.dot_general(
        left, right, (((0,), (0,)), ((), ())), preferred_element_type=jnp.float32
    )


def masked_scores(block_query, keys, pieces, first, scale_factor):
    count = block_query.shape[0]
    length = keys.shape[0]
    scores = (
        jnp.einsum("qgrd,kgd->grqk", block_query, keys, preferred_element_type=jnp.float32)
        * scale_factor
    )
    rows = first + jnp.arange(count)[:, None]
    columns = jnp.arange(length)[None, :]
    owner = pieces[first : first + count][:, None]
    allowed = (columns <= rows) | (owner == pieces[None, :]) & (owner != 0)
    return jnp.where(allowed, scores, -1e30)


def attend(query, keys, values, pieces, scale_factor):
    length = query.shape[0]
    block = min(512, length)
    attended_parts = []
    total_parts = []
    for first in range(0, length, block):
        scores = masked_scores(query[first : first + block], keys, pieces, first, scale_factor)
        peak = jnp.max(scores, axis=-1, keepdims=True)
        exponent = jnp.exp(scores - peak)
        total = jnp.sum(exponent, axis=-1, keepdims=True)
        probs = (exponent / total).astype(jnp.bfloat16)
        attended_parts.append(
            jnp.einsum("grqk,kgd->qgrd", probs, values, preferred_element_type=jnp.float32).astype(
                jnp.bfloat16
            )
        )
        total_parts.append(peak + jnp.log(total))
    return (jnp.concatenate(attended_parts, axis=0), jnp.concatenate(total_parts, axis=2))


def attend_back(query, keys, values, grad_attended, log_totals, pieces, scale_factor):
    length = query.shape[0]
    block = min(512, length)
    grad_query_parts = []
    grad_keys = jnp.zeros(keys.shape, jnp.float32)
    grad_values = jnp.zeros(values.shape, jnp.float32)
    for first in range(0, length, block):
        block_query = query[first : first + block]
        block_grad = grad_attended[first : first + block]
        scores = masked_scores(block_query, keys, pieces, first, scale_factor)
        probs = jnp.exp(scores - log_totals[:, :, first : first + block])
        probs_low = probs.astype(jnp.bfloat16)
        grad_probs = jnp.einsum(
            "qgrd,kgd->grqk", block_grad, values, preferred_element_type=jnp.float32
        )
        inner = jnp.sum(probs * grad_probs, axis=-1, keepdims=True)
        grad_scores = (probs * (grad_probs - inner)).astype(jnp.bfloat16)
        grad_query_parts.append(
            jnp.einsum("grqk,kgd->qgrd", grad_scores, keys, preferred_element_type=jnp.float32)
            * scale_factor
        )
        grad_keys = (
            grad_keys
            + jnp.einsum(
                "grqk,qgrd->kgd", grad_scores, block_query, preferred_element_type=jnp.float32
            )
            * scale_factor
        )
        grad_values = grad_values + jnp.einsum(
            "grqk,qgrd->kgd", probs_low, block_grad, preferred_element_type=jnp.float32
        )
    return (jnp.concatenate(grad_query_parts, axis=0), grad_keys, grad_values)


def exchange(value, axis, bit, size):
    return lax.ppermute(value, axis, [(i, i ^ (1 << bit)) for i in range(size)])


class Cube:
    def __init__(self, size):
        self.size = size
        self.bits = size.bit_length() - 1
        self.masks = [
            sum(((place >> (self.bits - 1 - k)) & 1) << k for k in range(self.bits))
            for place in range(size)
        ]
        self.near_last = list(range(self.bits - 1, -1, -1))
        self.near_first = [0] + list(range(self.bits - 1, 0, -1))

    def swap(self, value, bit):
        return exchange(value, "dp", bit, self.size)

    def gather(self, shard, order):
        have = {0: shard}
        for bit in order:
            for mask in list(have):
                have[mask | (1 << bit)] = self.swap(have[mask], bit)
        return [have[mask] for mask in self.masks]

    def gather_small(self, shard):
        have = shard
        for bit in self.near_last:
            have = jnp.concatenate([have, self.swap(have, bit)], axis=-1)
        return have

    def to_relative(self, rows):
        me = lax.axis_index("dp")
        width = rows.shape[1] // self.size
        return jnp.concatenate(
            [
                lax.dynamic_slice_in_dim(rows, (me ^ mask) * width, width, axis=1)
                for mask in self.masks
            ],
            axis=1,
        )

    def from_relative(self, rows):
        me = lax.axis_index("dp")
        width = rows.shape[1] // self.size
        mirror = sum(((me >> k) & 1) << (self.bits - 1 - k) for k in range(self.bits))
        return jnp.concatenate(
            [
                lax.dynamic_slice_in_dim(rows, (mirror ^ mask) * width, width, axis=1)
                for mask in self.masks
            ],
            axis=1,
        )

    def scatter(self, sent, kept, bit, axis, rest):
        total = kept.astype(jnp.float32) + self.swap(sent, bit).astype(jnp.float32)
        for bit in rest:
            half = total.shape[axis] // 2
            low = lax.slice_in_dim(total, 0, half, axis=axis)
            high = lax.slice_in_dim(total, half, 2 * half, axis=axis)
            total = low + self.swap(high.astype(jnp.bfloat16), bit).astype(jnp.float32)
        return total

    def halves(self, right, left, axis):
        if axis == 0:
            half = left.shape[1] // 2
            sent = across_rows(left[:, half:], right)
            kept = across_rows(left[:, :half], right)
        else:
            half = right.shape[1] // 2
            sent = across_rows(left, right[:, half:])
            kept = across_rows(left, right[:, :half])
        return sent.astype(jnp.bfloat16), kept

    def grad(self, left, right, axis):
        sent, kept = self.halves(right, left, axis)
        return self.scatter(sent, kept, 0, axis, range(1, self.bits))


def gather_tensor(rows):
    return lax.all_gather(rows, "tensor", axis=0, tiled=True)


def scatter_tensor(rows):
    return lax.psum_scatter(
        rows.astype(jnp.bfloat16), "tensor", scatter_dimension=0, tiled=True
    ).astype(jnp.float32)


def local(
    cube,
    tokens,
    pieces,
    positions,
    cotangent,
    attn_norm,
    w_query,
    w_key,
    w_value,
    w_out,
    mlp_norm,
    w_gate,
    w_up,
    w_down,
):
    low = jnp.bfloat16
    gains = cube.gather_small(jnp.stack([attn_norm, mlp_norm]).astype(low))
    attn_gain, mlp_gain = gains[0], gains[1]
    wide = w_query.shape[1]
    narrow = w_key.shape[1]
    packed = cube.gather(
        jnp.concatenate([w_query.astype(low), w_key.astype(low), w_value.astype(low)], axis=1),
        cube.near_first,
    )
    qkv_weight = jnp.concatenate(packed, axis=0)
    out_weight = jnp.concatenate(cube.gather(w_out.astype(low), cube.near_first), axis=1)
    gate_weight = jnp.concatenate(cube.gather(w_gate.astype(low), cube.near_last), axis=0)
    up_weight = jnp.concatenate(cube.gather(w_up.astype(low), cube.near_last), axis=0)
    down_weight = jnp.concatenate(cube.gather(w_down.astype(low), cube.near_last), axis=1)

    group = HEADS // KV_HEADS
    key_heads = narrow // HEAD_DIM
    scale_factor = HEAD_DIM ** (-0.5)
    residual = cube.to_relative(tokens).astype(jnp.float32)
    normed_one, inverse_one = normalize(residual, attn_gain)
    normed_full = gather_tensor(normed_one)
    length = normed_full.shape[0]
    angles = rotary_angles(positions, HEAD_DIM)
    projected = row_product(normed_full, qkv_weight)
    query = projected[:, :wide].reshape(length, -1, HEAD_DIM)
    query = rotate(query, angles).astype(low).reshape(length, key_heads, group, HEAD_DIM)
    keys = projected[:, wide : wide + narrow].reshape(length, key_heads, HEAD_DIM)
    keys = rotate(keys, angles).astype(low)
    values = projected[:, wide + narrow :].astype(low).reshape(length, key_heads, HEAD_DIM)
    attended, log_totals = attend(query, keys, values, pieces, scale_factor)
    attended_flat = attended.reshape(length, -1)
    middle = residual + scatter_tensor(row_product(attended_flat, out_weight))
    normed_two, inverse_two = normalize(middle, mlp_gain)
    normed_full_two = gather_tensor(normed_two)
    relative_grad = cube.to_relative(cotangent)
    grad_out = relative_grad.astype(jnp.float32)
    grad_out_full = gather_tensor(relative_grad)
    gate = row_product(normed_full_two, gate_weight)
    up = row_product(normed_full_two, up_weight)
    gate_sigmoid = jax.nn.sigmoid(gate)
    activated = gate * gate_sigmoid
    hidden = (activated * up).astype(low)
    grad_w_down = cube.grad(hidden, grad_out_full, 1)
    result = middle + scatter_tensor(row_product(hidden, down_weight))
    output = cube.from_relative(result.astype(low))
    grad_hidden = back_product((grad_out_full,), (down_weight,))
    grad_gate = (grad_hidden * up * gate_sigmoid * (1.0 + gate * (1.0 - gate_sigmoid))).astype(low)
    grad_up = (grad_hidden * activated).astype(low)
    grad_w_gate = cube.grad(normed_full_two, grad_gate, 0)
    grad_w_up = cube.grad(normed_full_two, grad_up, 0)
    grad_normed_two = scatter_tensor(back_product((grad_gate, grad_up), (gate_weight, up_weight)))
    grad_middle_norm, grad_gain_two = normalize_back(grad_normed_two, middle, inverse_two, mlp_gain)
    grad_middle = grad_out + grad_middle_norm
    grad_branch_full = gather_tensor(grad_middle.astype(low))
    grad_w_out = cube.grad(attended_flat, grad_branch_full, 1)
    grad_attended = back_product((grad_branch_full,), (out_weight,))
    grad_attended = grad_attended.astype(low).reshape(length, key_heads, group, HEAD_DIM)
    grad_query_rot, grad_keys_rot, grad_values = attend_back(
        query, keys, values, grad_attended, log_totals, pieces, scale_factor
    )
    grad_query = rotate(grad_query_rot.reshape(length, -1, HEAD_DIM), -angles).astype(low)
    grad_keys = rotate(grad_keys_rot, -angles).astype(low)
    grad_projected = jnp.concatenate(
        [
            grad_query.reshape(length, -1),
            grad_keys.reshape(length, -1),
            grad_values.astype(low).reshape(length, -1),
        ],
        axis=1,
    )
    grad_w_qkv = cube.grad(normed_full, grad_projected, 0)
    grad_normed_one = scatter_tensor(back_product((grad_projected,), (qkv_weight,)))
    grad_input_norm, grad_gain_one = normalize_back(
        grad_normed_one, residual, inverse_one, attn_gain
    )
    input_grad = cube.from_relative(grad_middle + grad_input_norm)
    gain_grads = lax.psum(jnp.stack([grad_gain_one, grad_gain_two]), "tensor")
    for bit in range(cube.bits):
        half = gain_grads.shape[1] // 2
        gain_grads = gain_grads[:, :half] + cube.swap(gain_grads[:, half:], bit)
    return (
        output,
        input_grad,
        gain_grads[0],
        grad_w_qkv[:, :wide],
        grad_w_qkv[:, wide : wide + narrow],
        grad_w_qkv[:, wide + narrow :],
        grad_w_out,
        gain_grads[1],
        grad_w_gate,
        grad_w_up,
        grad_w_down,
    )


def solution(mesh):
    return jax.shard_map(
        partial(local, Cube(mesh.shape["dp"])),
        mesh=mesh,
        in_specs=(
            P(("dp", "tensor"), None),
            P("dp"),
            P("dp"),
            P(("dp", "tensor"), None),
            P("dp"),
            P("dp", "tensor"),
            P("dp", "tensor"),
            P("dp", "tensor"),
            P("tensor", "dp"),
            P("dp"),
            P("dp", "tensor"),
            P("dp", "tensor"),
            P("tensor", "dp"),
        ),
        out_specs=(
            P(("dp", "tensor"), None),
            P(("dp", "tensor"), None),
            P("dp"),
            P("dp", "tensor"),
            P("dp", "tensor"),
            P("dp", "tensor"),
            P("tensor", "dp"),
            P("dp"),
            P("dp", "tensor"),
            P("dp", "tensor"),
            P("tensor", "dp"),
        ),
        check_vma=False,
    )
```
